32 devices in a mesh: farm: 2 (over y), clus: 4 (over x, core), lag: 4 (over z).
Axes of the slice: x: 2, y: 2, z: 4, core: 2. Of those that a mesh axis runs over, the one named last changes fastest.
Arguments:
- history: bfloat16 [8, 256, 2048], P(None, ('farm', 'lag'), 'clus'), parts along dimension 1, may hold values from -6 to 6
- kernel: bfloat16 [8, 2048, 2048], P('lag', 'clus'), may hold values from -0.046875 to 0.046875
- moments: bfloat16 [8, 8, 256], P(None, ('farm', 'clus')), parts along dimension 1, may hold values from -6 to 6
- coupling: bfloat16 [4, 3, 8, 256, 256], P('clus', None, 'lag'), may hold values from -0.078125 to 0.078125
- evaluation: float32 [256, 2048], replicated, may hold values from -0.375 to 0.375
- offsets: int32 [8], replicated, may hold values from 0 to 7, as said below
- pair_sources: int32 [4, 3], replicated, may hold values from 0 to 3, as said below
- body_cluster: int32 [128], replicated, may hold values from 0 to 3, as said below
Outputs:
- total: bfloat16 [256, 2048], P(('farm', 'lag'), 'clus'), parts along dimension 0
The draws below stay inside these ranges and needn't reach their ends.
There are 2 independent parts, one for each index of `farm`. The reference program is written for one: setup_inputs(seed, part) draws one part's arguments, and reference() takes and returns one part's arrays. A program takes and returns all parts, laid end to end along the dimension named above; an argument that names none is the same for every part. Nothing has to cross between parts.
Inputs may be any that keep to these rules, and one draw needn't show every extreme that they name: offsets lists every cycle slot exactly once. `pair_sources`: row d lists every cluster other than d exactly once. `body_cluster`: every cluster holds exactly 32 bodies.
All inputs are finite; a program needn't handle non-finite values.
Results may differ from the reference program's by a relative error of at most 0.0015.
Values may be sent and summed in bfloat16 or wider, within the bound.
No kernel may reach another device: no remote copies, remote signals or barrier semaphores. Data moves between devices by JAX's collectives and lax.ppermute only.
A program may use at most 64 MiB of HBM per device.

```python
import jax
import jax.numpy as jnp
from jax import lax

P_SIZE = 2048
M = 256
BPC = 32
LAGS = 8
CLUSTERS = 4
NP = 3
BODIES = 128


def draw_offsets(key, part):
    return jax.random.permutation(key, LAGS).astype(jnp.int32)


def draw_pair_sources(key, part):
    keys = jax.random.split(key, CLUSTERS)
    perms = jax.vmap(lambda one: jax.random.permutation(one, CLUSTERS - 1))(keys)
    dest = jnp.arange(CLUSTERS)[:, None]
    return (perms + (perms >= dest)).astype(jnp.int32)


def draw_body_cluster(key, part):
    labels = (jnp.arange(BODIES) // BPC).astype(jnp.int32)
    return jax.random.permutation(key, labels).astype(jnp.int32)


def steps_of(rng, dims, shards, smallest, high):
    factor_of = 1.0
    for axis_at, parts in shards:
        draws = jax.random.uniform(jax.random.fold_in(jax.random.fold_in(rng, 6), axis_at), (parts,), jnp.float32, smallest / len(shards), high / len(shards))
        factor_of = factor_of * jnp.repeat(jnp.exp(draws), dims[axis_at] // parts).reshape((-1,) + (1,) * (len(dims) - 1 - axis_at))
    return factor_of


def normal_values(key, shape, width, limit, shards=(), dtype=jnp.bfloat16):
    result = jax.random.normal(key, shape, jnp.float32) * width
    if len(shards) > 0:
        result = steps_of(key, shape, shards, -0.22, 0.18) * result
    return jnp.clip(result, min=-limit, max=limit).astype(dtype)


def setup_inputs(seed: int = 0, part: int = 0) -> dict:
    seeds = jax.random.split(jax.random.key(seed), 9)
    own_keys = jax.random.split(jax.random.fold_in(seeds[8], part), 9)
    return {
        "history": normal_values(own_keys[0], (LAGS, BODIES, P_SIZE), 1.0, 6.0, ((1, 4), (2, 4))),
        "kernel": normal_values(seeds[1], (LAGS, P_SIZE, P_SIZE), (LAGS * P_SIZE) ** -0.5, 0.046875, ((0, 4), (1, 4))),
        "moments": normal_values(own_keys[2], (LAGS, CLUSTERS, M), 1.0, 6.0, ((1, 4),)),
        "coupling": normal_values(seeds[3], (CLUSTERS, NP, LAGS, M, M), (NP * LAGS * M) ** -0.5, 0.078125, ((0, 4), (2, 4))),
        "evaluation": normal_values(seeds[4], (M, P_SIZE), M ** -0.5, 0.375, (), jnp.float32),
        "offsets": draw_offsets(jax.random.fold_in(seeds[8], 71), part),
        "pair_sources": draw_pair_sources(jax.random.fold_in(seeds[8], 71), part),
        "body_cluster": draw_body_cluster(jax.random.fold_in(seeds[8], 71), part),
    }


def reference(history, kernel, moments, coupling, evaluation, offsets, pair_sources, body_cluster):
    hist_type = jnp.float32

    def lag_step(accum, lag_id):
        slot = offsets[lag_id]
        rows = history[slot].astype(hist_type)
        weights = kernel[lag_id].astype(hist_type)
        return accum + jnp.dot(rows, weights, precision=lax.Precision.HIGHEST), None

    start = jnp.zeros((history.shape[1], history.shape[2]), hist_type)
    self_field, _ = lax.scan(lag_step, start, jnp.arange(offsets.shape[0]).astype(jnp.int32))
    picked = moments[offsets].astype(jnp.float32)

    def one_cluster(index):
        sources = pair_sources[index]
        source_moments = picked[:, sources, :]
        mats = coupling[index].astype(jnp.float32)
        return jnp.einsum('klmn,lkn->m', mats, source_moments, precision=lax.Precision.HIGHEST)

    local = lax.map(one_cluster, jnp.arange(pair_sources.shape[0]).astype(jnp.int32))
    far = jnp.dot(local, evaluation, precision=lax.Precision.HIGHEST)
    total = self_field + far[body_cluster]
    return total.astype(jnp.bfloat16)
```

```python
import jax
import jax.numpy as jnp
from jax import lax
from jax.experimental import pallas as pl
from jax.experimental.pallas import tpu as pltpu
from jax.sharding import PartitionSpec as P

F32 = jnp.float32
HBM = pl.BlockSpec(memory_space=pl.ANY)
VM = pl.BlockSpec(memory_space=pltpu.VMEM)
SM = pl.BlockSpec(memory_space=pltpu.SMEM)


def swap(value, axis, bit):
    count = lax.axis_size(axis)
    return lax.ppermute(value, axis, [(i, i ^ bit) for i in range(count)])


def pick_slots(history, offsets, lag_count, lags_here):
    shape = (lags_here,) + history.shape[1:]

    def body(offsets_ref, history_ref, *rest):
        outs, sems = rest[:lag_count], rest[lag_count]
        me = lax.axis_index("lag")
        copies = []
        for s in range(lag_count):
            for j in range(lags_here):
                slot = offsets_ref[(me ^ s) * lags_here + j]
                copies.append(
                    pltpu.make_async_copy(history_ref.at[slot], outs[s].at[j], sems.at[s, j])
                )
        for copy in copies:
            copy.start()
        for copy in copies:
            copy.wait()

    return pl.pallas_call(
        body,
        out_shape=[jax.ShapeDtypeStruct(shape, history.dtype)] * lag_count,
        in_specs=[SM, HBM],
        out_specs=[HBM] * lag_count,
        scratch_shapes=[pltpu.SemaphoreType.DMA((lag_count, lags_here))],
        name="pick_slots",
    )(offsets, history)


def far_rows(moments, coupling, evaluation, offsets, pair_sources, lags_here, blocks):
    width = evaluation.shape[1] // blocks
    sources = coupling.shape[0]
    terms = evaluation.shape[0]

    def body(offsets_ref, pairs_ref, moments_ref, coupling_ref, evaluation_ref, out_ref):
        lag = lax.axis_index("lag")
        clus = lax.axis_index("clus")
        total = jnp.zeros(coupling_ref.shape[2:], F32)
        for j in range(lags_here):
            slot = offsets_ref[lag * lags_here + j]
            for k in range(sources):
                rows = moments_ref[pairs_ref[clus, k] ^ clus].astype(F32)
                hit = lax.broadcasted_iota(jnp.int32, rows.shape, 0) == slot
                row = jnp.sum(jnp.where(hit, rows, 0.0), axis=0, keepdims=True)
                total += coupling_ref[k, j].astype(F32) * row
        local = jnp.sum(total, axis=1, keepdims=True)
        for t in range(blocks):
            start = pl.multiple_of((clus ^ t) * width, width)
            block = evaluation_ref[:, pl.ds(start, width)]
            out_ref[t : t + 1, :] = jnp.sum(block * local, axis=0, keepdims=True)

    return pl.pallas_call(
        body,
        out_shape=jax.ShapeDtypeStruct((blocks, width), F32),
        in_specs=[SM, SM, VM, VM, VM],
        out_specs=VM,
        cost_estimate=pl.CostEstimate(
            flops=2 * terms * evaluation.shape[1], bytes_accessed=4 << 20, transcendentals=0
        ),
        name="far_rows",
    )(offsets, pair_sources, moments, coupling, evaluation)


def partial_sums(pieces, kernel, far, body_cluster, blocks):
    lag_count = len(pieces)
    lags_here, here, depth = pieces[0].shape
    rows = lag_count * here
    width = kernel.shape[2] // blocks

    def body(clusters_ref, far_ref, kernel_ref, *rest):
        pieces_ref, keep_ref, send_ref = rest[:lag_count], rest[lag_count], rest[lag_count + 1]
        lag = lax.axis_index("lag")
        clus = lax.axis_index("clus")
        row = lax.broadcasted_iota(jnp.int32, (rows, rows), 0)
        column = lax.broadcasted_iota(jnp.int32, (rows, rows), 1)
        body_of_row = ((row // here) ^ lag) * here + row % here
        chosen = (column == body_of_row) & (clusters_ref[...] == clus)
        mask = jnp.sum(chosen.astype(F32), axis=1, keepdims=True)
        lhs = [
            jnp.concatenate([piece[j] for piece in pieces_ref], axis=0) for j in range(lags_here)
        ]
        for t in range(blocks):
            start = pl.multiple_of((clus ^ t) * width, width)
            total = mask * far_ref[t : t + 1, :]
            for j in range(lags_here):
                total += jnp.dot(
                    lhs[j], kernel_ref[j, :, pl.ds(start, width)], preferred_element_type=F32
                )
            out_ref = send_ref if t % 2 else keep_ref
            out_ref[:, (t // 2) * width : (t // 2 + 1) * width] = total

    half = jax.ShapeDtypeStruct((rows, width * (blocks // 2)), F32)
    return pl.pallas_call(
        body,
        out_shape=[half, half],
        in_specs=[VM] * (3 + lag_count),
        out_specs=[VM, VM],
        cost_estimate=pl.CostEstimate(
            flops=2 * rows * lags_here * depth * kernel.shape[2],
            bytes_accessed=kernel.size * 2 + 8 * half.size,
            transcendentals=0,
        ),
        name="partial_sums",
    )(body_cluster[None, :], far, kernel, *pieces)


def shards(history, kernel, moments, coupling, evaluation, offsets, pair_sources, body_cluster):
    lag_count = lax.axis_size("lag")
    blocks = lax.axis_size("clus")
    lags_here = kernel.shape[0]
    here = history.shape[1]
    width = history.shape[2]

    pieces = pick_slots(history, offsets, lag_count, lags_here)
    pieces = [pieces[0]] + [swap(pieces[s], "lag", s) for s in range(1, lag_count)]

    gathered = jnp.swapaxes(moments, 0, 1)
    bit = 1
    while bit < blocks:
        gathered = jnp.concatenate([gathered, swap(gathered, "clus", bit)], axis=0)
        bit *= 2
    far = far_rows(gathered, coupling[0], evaluation, offsets, pair_sources, lags_here, blocks)

    keep, send = partial_sums(pieces, kernel, far, body_cluster, blocks)
    bit = 1
    while True:
        came = swap(send, "clus", bit)
        bit *= 2
        if bit >= blocks:
            mine = keep + came
            break
        total = (keep + came).reshape(keep.shape[0], -1, 2, width)
        keep = total[:, :, 0].reshape(keep.shape[0], -1)
        send = total[:, :, 1].reshape(keep.shape[0], -1)
    parts = [mine[s * here : (s + 1) * here] for s in range(lag_count)]
    came = [swap(parts[s], "lag", s) for s in range(1, lag_count)]
    owned = parts[0]
    for value in came:
        owned = owned + value
    return owned.astype(jnp.bfloat16)


def solution(mesh):
    in_specs = (
        P(None, ("farm", "lag"), "clus"),
        P("lag", "clus", None),
        P(None, ("farm", "clus"), None),
        P("clus", None, "lag", None, None),
        P(),
        P(),
        P(),
        P(),
    )
    out_specs = P(("farm", "lag"), "clus")
    return jax.shard_map(shards, mesh=mesh, in_specs=in_specs, out_specs=out_specs, check_vma=False)
```

```python
import jax
import jax.numpy as jnp
from jax import lax
from jax.experimental import pallas as pl
from jax.experimental.pallas import tpu as pltpu
from jax.sharding import PartitionSpec as P

F32 = jnp.float32
HBM = pl.BlockSpec(memory_space=pltpu.HBM)
VM = pl.BlockSpec(memory_space=pltpu.VMEM)
SM = pl.BlockSpec(memory_space=pltpu.SMEM)
LIMIT = 16 << 20


def swap(value, axis, bit):
    count = lax.axis_size(axis)
    return lax.ppermute(value, axis, [(i, i ^ bit) for i in range(count)])


def in_vmem(value):
    return pltpu.with_memory_space_constraint(value, pltpu.VMEM)


def in_hbm(value):
    return pltpu.with_memory_space_constraint(value, pltpu.HBM)


def pick_slots(history, moments, offsets, lag_count, lags_here):
    shape = (lags_here,) + history.shape[1:]

    def body(offsets_ref, history_ref, moments_ref, *rest):
        outs, moments_out = rest[:lag_count], rest[lag_count]
        sems, moments_sem = rest[lag_count + 1 :]
        me = lax.axis_index("lag")
        copies = [pltpu.make_async_copy(moments_ref, moments_out, moments_sem)]
        for s in range(lag_count):
            for j in range(lags_here):
                slot = offsets_ref[(me ^ s) * lags_here + j]
                copies.append(
                    pltpu.make_async_copy(history_ref.at[slot], outs[s].at[j], sems.at[s, j])
                )
        for copy in copies:
            copy.start()
        for copy in copies:
            copy.wait()

    return pl.pallas_call(
        body,
        out_shape=[pltpu.VMEM(shape, history.dtype)] * lag_count
        + [pltpu.VMEM(moments.shape, moments.dtype)],
        in_specs=[SM, HBM, HBM],
        out_specs=[VM] * (lag_count + 1),
        scratch_shapes=[
            pltpu.SemaphoreType.DMA((lag_count, lags_here)),
            pltpu.SemaphoreType.DMA,
        ],
        compiler_params=pltpu.CompilerParams(vmem_limit_bytes=LIMIT),
        name="pick_slots",
    )(in_hbm(offsets), in_hbm(history), in_hbm(moments))


def far_rows(moments, coupling, evaluation, kernel, offsets, pair_sources, body_cluster, here):
    blocks = len(moments)
    width = evaluation.shape[1] // blocks
    sources, lags_here = coupling.shape[:2]
    terms = evaluation.shape[0]
    slots = moments[0].shape[0]
    rows = body_cluster.shape[1]

    def body(offsets_ref, pairs_ref, clusters_ref, coupling_hbm, evaluation_hbm, kernel_hbm, *rest):
        moments_refs = rest[:blocks]
        out_ref, mask_ref, kernel_ref, coupling_ref, evaluation_ref, sems = rest[blocks:]
        copies = [
            pltpu.make_async_copy(coupling_hbm, coupling_ref, sems.at[0]),
            pltpu.make_async_copy(evaluation_hbm, evaluation_ref, sems.at[1]),
            pltpu.make_async_copy(kernel_hbm, kernel_ref, sems.at[2]),
        ]
        for copy in copies:
            copy.start()
        lag = lax.axis_index("lag")
        clus = lax.axis_index("clus")
        row = lax.broadcasted_iota(jnp.int32, (rows, rows), 0)
        column = lax.broadcasted_iota(jnp.int32, (rows, rows), 1)
        body_of_row = ((row // here) ^ lag) * here + row % here
        chosen = (column == body_of_row) & (clusters_ref[...] == clus)
        mask_ref[...] = jnp.sum(chosen.astype(F32), axis=1, keepdims=True)
        slot_of = lax.broadcasted_iota(jnp.int32, (slots, terms), 0)
        values = [ref[...].astype(F32) for ref in moments_refs]
        wanted = []
        for k in range(sources):
            place = pairs_ref[clus, k] ^ clus
            found = values[0]
            for t in range(1, blocks):
                found = jnp.where(place == t, values[t], found)
            for j in range(lags_here):
                slot = offsets_ref[lag * lags_here + j]
                wanted.append(
                    jnp.sum(jnp.where(slot_of == slot, found, 0.0), axis=0, keepdims=True)
                )
        copies[0].wait()
        total = jnp.zeros(coupling_ref.shape[2:], F32)
        for k in range(sources):
            for j in range(lags_here):
                total += coupling_ref[k, j].astype(F32) * wanted[k * lags_here + j]
        local = jnp.sum(total, axis=1, keepdims=True)
        copies[1].wait()
        for t in range(blocks):
            start = pl.multiple_of((clus ^ t) * width, width)
            block = evaluation_ref[:, pl.ds(start, width)]
            out_ref[t : t + 1, :] = jnp.sum(block * local, axis=0, keepdims=True)
        copies[2].wait()

    return pl.pallas_call(
        body,
        out_shape=[
            pltpu.VMEM((blocks, width), F32),
            pltpu.VMEM((rows, 1), F32),
            pltpu.VMEM(kernel.shape, kernel.dtype),
        ],
        in_specs=[SM, SM, VM, HBM, HBM, HBM] + [VM] * blocks,
        out_specs=[VM, VM, VM],
        scratch_shapes=[
            pltpu.VMEM(coupling.shape, coupling.dtype),
            pltpu.VMEM(evaluation.shape, evaluation.dtype),
            pltpu.SemaphoreType.DMA((3,)),
        ],
        compiler_params=pltpu.CompilerParams(vmem_limit_bytes=LIMIT),
        cost_estimate=pl.CostEstimate(
            flops=2 * terms * evaluation.shape[1], bytes_accessed=7 << 20, transcendentals=0
        ),
        name="far_rows",
    )(
        in_hbm(offsets),
        in_hbm(pair_sources),
        in_hbm(body_cluster),
        in_hbm(coupling),
        in_hbm(evaluation),
        in_hbm(kernel),
        *[in_vmem(value) for value in moments],
    )


def partial_sums(pieces, kernel, far, mask):
    lag_count = len(pieces)
    lags_here, here, depth = pieces[0].shape
    rows = lag_count * here
    blocks, width = far.shape

    def body(mask_ref, far_ref, kernel_ref, *rest):
        pieces_ref, keep_ref, send_ref = rest[:lag_count], rest[lag_count], rest[lag_count + 1]
        clus = lax.axis_index("clus")
        mask = mask_ref[...]
        lhs = [
            jnp.concatenate([piece[j] for piece in pieces_ref], axis=0) for j in range(lags_here)
        ]
        for t in range(blocks):
            start = pl.multiple_of((clus ^ t) * width, width)
            total = mask * far_ref[t : t + 1, :]
            for j in range(lags_here):
                total += jnp.dot(
                    lhs[j], kernel_ref[j, :, pl.ds(start, width)], preferred_element_type=F32
                )
            out_ref = send_ref if t % 2 else keep_ref
            out_ref[t // 2] = total

    half = pltpu.VMEM((blocks // 2, rows, width), F32)
    return pl.pallas_call(
        body,
        out_shape=[half, half],
        in_specs=[VM] * (3 + lag_count),
        out_specs=[VM, VM],
        compiler_params=pltpu.CompilerParams(vmem_limit_bytes=LIMIT),
        cost_estimate=pl.CostEstimate(
            flops=2 * rows * lags_here * depth * kernel.shape[2],
            bytes_accessed=kernel.size * 2 + 4 * rows * width * blocks,
            transcendentals=0,
        ),
        name="partial_sums",
    )(in_vmem(mask), in_vmem(far), in_vmem(kernel), *[in_vmem(piece) for piece in pieces])


def shards(history, kernel, moments, coupling, evaluation, offsets, pair_sources, body_cluster):
    lag_count = lax.axis_size("lag")
    clus_count = lax.axis_size("clus")
    lags_here = kernel.shape[0]
    here = history.shape[1]

    *pieces, mine = pick_slots(history, moments[:, 0], offsets, lag_count, lags_here)
    pieces = [pieces[0]] + [swap(pieces[s], "lag", s) for s in range(1, lag_count)]
    gathered = [mine] + [swap(mine, "clus", t) for t in range(1, clus_count)]
    far, mask, near = far_rows(
        gathered, coupling[0], evaluation, kernel, offsets, pair_sources, body_cluster[None], here
    )

    keep, send = partial_sums(pieces, near, far, mask)
    kept = [keep[i] for i in range(clus_count // 2)]
    came = swap(send, "clus", 1)
    kept = [kept[i] + came[i] for i in range(clus_count // 2)]
    bit = 2
    while bit < clus_count:
        came = [swap(value, "clus", bit) for value in kept[1::2]]
        kept = [a + b for a, b in zip(kept[0::2], came)]
        bit *= 2
    parts = [kept[0][s * here : (s + 1) * here] for s in range(lag_count)]
    owned = parts[0]
    for s in range(1, lag_count):
        owned = owned + swap(parts[s], "lag", s)
    return owned.astype(jnp.bfloat16)


def solution(mesh):
    in_specs = (
        P(None, ("farm", "lag"), "clus"),
        P("lag", "clus", None),
        P(None, ("farm", "clus"), None),
        P("clus", None, "lag", None, None),
        P(),
        P(),
        P(),
        P(),
    )
    out_specs = P(("farm", "lag"), "clus")
    return jax.shard_map(shards, mesh=mesh, in_specs=in_specs, out_specs=out_specs, check_vma=False)
```

```python
import jax
import jax.numpy as jnp
from jax import lax
from jax.experimental import pallas as pl
from jax.experimental.pallas import tpu as pltpu
from jax.sharding import PartitionSpec as P

F32 = jnp.float32
HBM = pl.BlockSpec(memory_space=pltpu.HBM)
VM = pl.BlockSpec(memory_space=pltpu.VMEM)
SM = pl.BlockSpec(memory_space=pltpu.SMEM)
LIMIT = 16 << 20


def swap(value, axis, bit):
    count = lax.axis_size(axis)
    return lax.ppermute(value, axis, [(i, i ^ bit) for i in range(count)])


def in_vmem(value):
    return pltpu.with_memory_space_constraint(value, pltpu.VMEM)


def in_hbm(value):
    return pltpu.with_memory_space_constraint(value, pltpu.HBM)


def pick_slots(history, moments, offsets, lag_count, lags_here):
    shape = (lags_here,) + history.shape[1:]

    def body(offsets_ref, history_ref, moments_ref, *rest):
        outs, moments_out = rest[:lag_count], rest[lag_count]
        sems, moments_sem = rest[lag_count + 1 :]
        me = lax.axis_index("lag")
        copies = [pltpu.make_async_copy(moments_ref, moments_out, moments_sem)]
        for s in range(lag_count):
            for j in range(lags_here):
                slot = offsets_ref[(me ^ s) * lags_here + j]
                copies.append(
                    pltpu.make_async_copy(history_ref.at[slot], outs[s].at[j], sems.at[s, j])
                )
        for copy in copies:
            copy.start()
        for copy in copies:
            copy.wait()

    return pl.pallas_call(
        body,
        out_shape=[pltpu.VMEM(shape, history.dtype)] * lag_count
        + [pltpu.VMEM(moments.shape, moments.dtype)],
        in_specs=[SM, HBM, HBM],
        out_specs=[VM] * (lag_count + 1),
        scratch_shapes=[
            pltpu.SemaphoreType.DMA((lag_count, lags_here)),
            pltpu.SemaphoreType.DMA,
        ],
        compiler_params=pltpu.CompilerParams(vmem_limit_bytes=LIMIT),
        name="pick_slots",
    )(in_hbm(offsets), in_hbm(history), in_hbm(moments))


def bring_near(arrived, arrays, offsets, pair_sources, body_cluster, here, lags_here):
    count = len(arrays)
    rows = body_cluster.shape[1]
    slots = offsets.shape[1]
    blocks, sources = pair_sources.shape

    def body(arrived_ref, offsets_hbm, pairs_hbm, clusters_hbm, *rest):
        sources_hbm, outs = rest[:count], rest[count : 2 * count]
        mask_ref, picks_ref, offsets_ref, pairs_ref, clusters_ref, sems = rest[2 * count :]
        copies = [
            pltpu.make_async_copy(offsets_hbm, offsets_ref, sems.at[0]),
            pltpu.make_async_copy(pairs_hbm, pairs_ref, sems.at[1]),
            pltpu.make_async_copy(clusters_hbm, clusters_ref, sems.at[2]),
        ]
        for i in range(count):
            copies.append(pltpu.make_async_copy(sources_hbm[i], outs[i], sems.at[3 + i]))
        for copy in copies:
            copy.start()
        for copy in copies[:3]:
            copy.wait()
        lag = lax.axis_index("lag")
        clus = lax.axis_index("clus")
        row = lax.broadcasted_iota(jnp.int32, (rows, rows), 0)
        column = lax.broadcasted_iota(jnp.int32, (rows, rows), 1)
        body_of_row = ((row // here) ^ lag) * here + row % here
        chosen = (column == body_of_row) & (clusters_ref[...] == clus)
        mask_ref[...] = jnp.sum(chosen.astype(F32), axis=1, keepdims=True)
        place = lax.broadcasted_iota(jnp.int32, (1, blocks * slots), 1)
        lag_at = lax.broadcasted_iota(jnp.int32, (1, slots), 1)
        pair_row = lax.broadcasted_iota(jnp.int32, (blocks, sources), 0)
        pair_at = lax.broadcasted_iota(jnp.int32, (blocks, sources), 1)
        offsets = offsets_ref[...]
        pairs = pairs_ref[...]
        for j in range(lags_here):
            slot = jnp.where(lag_at == lag * lags_here + j, offsets, 0)
            slot = jnp.sum(slot, axis=1, keepdims=True)
            for k in range(sources):
                source = jnp.where((pair_row == clus) & (pair_at == k), pairs, 0)
                source = jnp.sum(jnp.sum(source, axis=1, keepdims=True), axis=0, keepdims=True)
                at = (source ^ clus) * slots + slot
                r = k * lags_here + j
                picks_ref[r : r + 1, :] = (place == at).astype(F32)
        for copy in copies[3:]:
            copy.wait()

    return pl.pallas_call(
        body,
        out_shape=[pltpu.VMEM(a.shape, a.dtype) for a in arrays]
        + [pltpu.VMEM((rows, 1), F32), pltpu.VMEM((sources * lags_here, blocks * slots), F32)],
        in_specs=[VM] + [HBM] * (count + 3),
        out_specs=[VM] * (count + 2),
        scratch_shapes=[
            pltpu.VMEM(offsets.shape, jnp.int32),
            pltpu.VMEM(pair_sources.shape, jnp.int32),
            pltpu.VMEM(body_cluster.shape, jnp.int32),
            pltpu.SemaphoreType.DMA((count + 3,)),
        ],
        compiler_params=pltpu.CompilerParams(vmem_limit_bytes=LIMIT),
        cost_estimate=pl.CostEstimate(flops=0, bytes_accessed=7 << 20, transcendentals=0),
        name="bring_near",
    )(
        in_vmem(arrived),
        in_hbm(offsets),
        in_hbm(pair_sources),
        in_hbm(body_cluster),
        *[in_hbm(a) for a in arrays],
    )


def far_rows(moments, picks, coupling, evaluation):
    blocks = len(moments)
    width = evaluation.shape[1] // blocks
    sources, lags_here = coupling.shape[:2]
    terms = evaluation.shape[0]

    def body(picks_ref, coupling_ref, evaluation_ref, *rest):
        moments_refs, out_ref = rest[:blocks], rest[blocks]
        clus = lax.axis_index("clus")
        values = jnp.concatenate([ref[...].astype(F32) for ref in moments_refs], axis=0)
        wanted = jnp.dot(
            picks_ref[...].astype(jnp.bfloat16),
            values.astype(jnp.bfloat16),
            preferred_element_type=F32,
        )
        total = jnp.zeros(coupling_ref.shape[2:], F32)
        for k in range(sources):
            for j in range(lags_here):
                r = k * lags_here + j
                total += coupling_ref[k, j].astype(F32) * wanted[r : r + 1, :]
        local = jnp.sum(total, axis=1, keepdims=True)
        for t in range(blocks):
            start = pl.multiple_of((clus ^ t) * width, width)
            block = evaluation_ref[:, pl.ds(start, width)]
            out_ref[t : t + 1, :] = jnp.sum(block * local, axis=0, keepdims=True)

    return pl.pallas_call(
        body,
        out_shape=pltpu.VMEM((blocks, width), F32),
        in_specs=[VM] * (3 + blocks),
        out_specs=VM,
        compiler_params=pltpu.CompilerParams(vmem_limit_bytes=LIMIT),
        cost_estimate=pl.CostEstimate(
            flops=2 * terms * evaluation.shape[1], bytes_accessed=3 << 20, transcendentals=0
        ),
        name="far_rows",
    )(in_vmem(picks), in_vmem(coupling), in_vmem(evaluation), *[in_vmem(v) for v in moments])


def partial_sums(pieces, kernel, far, mask):
    lag_count = len(pieces)
    lags_here, here, depth = pieces[0].shape
    rows = lag_count * here
    blocks, width = far.shape

    def body(mask_ref, far_ref, kernel_ref, *rest):
        keep_ref, send_ref = rest[lag_count], rest[lag_count + 1]
        pieces_ref = (rest[0],) + rest[lag_count - 1 : 0 : -1]
        clus = lax.axis_index("clus")
        mask = mask_ref[...]
        lhs = [
            jnp.concatenate([piece[j] for piece in pieces_ref], axis=0) for j in range(lags_here)
        ]
        for t in range(blocks):
            start = pl.multiple_of((clus ^ t) * width, width)
            total = mask * far_ref[t : t + 1, :]
            for j in range(lags_here):
                total += jnp.dot(
                    lhs[j], kernel_ref[j, :, pl.ds(start, width)], preferred_element_type=F32
                )
            out_ref = send_ref if t % 2 else keep_ref
            out_ref[t // 2] = total

    half = pltpu.VMEM((blocks // 2, rows, width), F32)
    return pl.pallas_call(
        body,
        out_shape=[half, half],
        in_specs=[VM] * (3 + lag_count),
        out_specs=[VM, VM],
        compiler_params=pltpu.CompilerParams(vmem_limit_bytes=LIMIT),
        cost_estimate=pl.CostEstimate(
            flops=2 * rows * lags_here * depth * kernel.shape[2],
            bytes_accessed=kernel.size * 2 + 4 * rows * width * blocks,
            transcendentals=0,
        ),
        name="partial_sums",
    )(in_vmem(mask), in_vmem(far), in_vmem(kernel), *[in_vmem(pieces[-s]) for s in range(lag_count)])


def shards(history, kernel, moments, coupling, evaluation, offsets, pair_sources, body_cluster):
    lag_count = lax.axis_size("lag")
    clus_count = lax.axis_size("clus")
    lags_here = kernel.shape[0]
    here = history.shape[1]

    *pieces, mine = pick_slots(history, moments[:, 0], offsets, lag_count, lags_here)
    pieces = [pieces[0]] + [swap(pieces[s], "lag", s) for s in range(1, lag_count)]
    gathered = [mine] + [swap(mine, "clus", t) for t in range(1, clus_count)]
    near, coupling_near, evaluation_near, mask, picks = bring_near(
        gathered[1],
        [kernel, coupling[0], evaluation],
        offsets[None],
        pair_sources,
        body_cluster[None],
        here,
        lags_here,
    )
    far = far_rows(gathered, picks, coupling_near, evaluation_near)

    keep, send = partial_sums(pieces, near, far, mask)
    kept = [keep[i] for i in range(clus_count // 2)]
    came = swap(send, "clus", 1)
    kept = [kept[i] + came[i] for i in range(clus_count // 2)]
    bit = 2
    while bit < clus_count:
        came = [swap(value, "clus", bit) for value in kept[1::2]]
        kept = [a + b for a, b in zip(kept[0::2], came)]
        bit *= 2
    parts = [kept[0][s * here : (s + 1) * here] for s in range(lag_count)]
    owned = parts[0]
    for s in [lag_count - 1] + list(range(1, lag_count - 1)):
        owned = owned + swap(parts[s], "lag", s)
    return owned.astype(jnp.bfloat16)


def solution(mesh):
    in_specs = (
        P(None, ("farm", "lag"), "clus"),
        P("lag", "clus", None),
        P(None, ("farm", "clus"), None),
        P("clus", None, "lag", None, None),
        P(),
        P(),
        P(),
        P(),
    )
    out_specs = P(("farm", "lag"), "clus")
    return jax.shard_map(shards, mesh=mesh, in_specs=in_specs, out_specs=out_specs, check_vma=False)
```

```python
import jax
import jax.numpy as jnp
from jax import lax
from jax.experimental import pallas as pl
from jax.experimental.pallas import tpu as pltpu
from jax.sharding import PartitionSpec as P

F32 = jnp.float32
HBM = pl.BlockSpec(memory_space=pltpu.HBM)
VM = pl.BlockSpec(memory_space=pltpu.VMEM)
SM = pl.BlockSpec(memory_space=pltpu.SMEM)
LIMIT = 16 << 20


def swap(value, axis, bit):
    count = lax.axis_size(axis)
    return lax.ppermute(value, axis, [(i, i ^ bit) for i in range(count)])


def in_vmem(value):
    return pltpu.with_memory_space_constraint(value, pltpu.VMEM)


def in_hbm(value):
    return pltpu.with_memory_space_constraint(value, pltpu.HBM)


def pick_slots(history, moments, offsets, lag_count, lags_here):
    shape = (lags_here,) + history.shape[1:]

    def body(offsets_ref, history_ref, moments_ref, *rest):
        outs, moments_out = rest[:lag_count], rest[lag_count]
        sems, moments_sem = rest[lag_count + 1 :]
        me = lax.axis_index("lag")
        copies = [pltpu.make_async_copy(moments_ref, moments_out, moments_sem)]
        for s in range(lag_count):
            for j in range(lags_here):
                slot = offsets_ref[(me ^ s) * lags_here + j]
                copies.append(
                    pltpu.make_async_copy(history_ref.at[slot], outs[s].at[j], sems.at[s, j])
                )
        for copy in copies:
            copy.start()
        for copy in copies:
            copy.wait()

    return pl.pallas_call(
        body,
        out_shape=[pltpu.VMEM(shape, history.dtype)] * lag_count
        + [pltpu.VMEM(moments.shape, moments.dtype)],
        in_specs=[SM, HBM, HBM],
        out_specs=[VM] * (lag_count + 1),
        scratch_shapes=[
            pltpu.SemaphoreType.DMA((lag_count, lags_here)),
            pltpu.SemaphoreType.DMA,
        ],
        compiler_params=pltpu.CompilerParams(vmem_limit_bytes=LIMIT),
        name="pick_slots",
    )(in_hbm(offsets), in_hbm(history), in_hbm(moments))


def bring_near(arrived, arrays, offsets, pair_sources, body_cluster, here, lags_here):
    count = len(arrays)
    rows = body_cluster.shape[1]
    slots = offsets.shape[1]
    blocks, sources = pair_sources.shape

    def body(arrived_ref, offsets_hbm, pairs_hbm, clusters_hbm, *rest):
        sources_hbm, outs = rest[:count], rest[count : 2 * count]
        mask_ref, picks_ref, offsets_ref, pairs_ref, clusters_ref, sems = rest[2 * count :]
        copies = [
            pltpu.make_async_copy(offsets_hbm, offsets_ref, sems.at[0]),
            pltpu.make_async_copy(pairs_hbm, pairs_ref, sems.at[1]),
            pltpu.make_async_copy(clusters_hbm, clusters_ref, sems.at[2]),
        ]
        for i in range(count):
            copies.append(pltpu.make_async_copy(sources_hbm[i], outs[i], sems.at[3 + i]))
        for copy in copies:
            copy.start()
        for copy in copies[:3]:
            copy.wait()
        lag = lax.axis_index("lag")
        clus = lax.axis_index("clus")
        row = lax.broadcasted_iota(jnp.int32, (rows, rows), 0)
        column = lax.broadcasted_iota(jnp.int32, (rows, rows), 1)
        body_of_row = ((row // here) ^ lag) * here + row % here
        chosen = (column == body_of_row) & (clusters_ref[...] == clus)
        mask_ref[...] = jnp.sum(chosen.astype(F32), axis=1, keepdims=True)
        place = lax.broadcasted_iota(jnp.int32, (1, blocks * slots), 1)
        lag_at = lax.broadcasted_iota(jnp.int32, (1, slots), 1)
        pair_row = lax.broadcasted_iota(jnp.int32, (blocks, sources), 0)
        pair_at = lax.broadcasted_iota(jnp.int32, (blocks, sources), 1)
        offsets = offsets_ref[...]
        pairs = pairs_ref[...]
        for j in range(lags_here):
            slot = jnp.where(lag_at == lag * lags_here + j, offsets, 0)
            slot = jnp.sum(slot, axis=1, keepdims=True)
            for k in range(sources):
                source = jnp.where((pair_row == clus) & (pair_at == k), pairs, 0)
                source = jnp.sum(jnp.sum(source, axis=1, keepdims=True), axis=0, keepdims=True)
                at = (source ^ clus) * slots + slot
                r = k * lags_here + j
                picks_ref[r : r + 1, :] = (place == at).astype(F32)
        for copy in copies[3:]:
            copy.wait()

    return pl.pallas_call(
        body,
        out_shape=[pltpu.VMEM(a.shape, a.dtype) for a in arrays]
        + [pltpu.VMEM((rows, 1), F32), pltpu.VMEM((sources * lags_here, blocks * slots), F32)],
        in_specs=[VM] + [HBM] * (count + 3),
        out_specs=[VM] * (count + 2),
        scratch_shapes=[
            pltpu.VMEM(offsets.shape, jnp.int32),
            pltpu.VMEM(pair_sources.shape, jnp.int32),
            pltpu.VMEM(body_cluster.shape, jnp.int32),
            pltpu.SemaphoreType.DMA((count + 3,)),
        ],
        compiler_params=pltpu.CompilerParams(vmem_limit_bytes=LIMIT),
        cost_estimate=pl.CostEstimate(flops=0, bytes_accessed=7 << 20, transcendentals=0),
        name="bring_near",
    )(
        in_vmem(arrived),
        in_hbm(offsets),
        in_hbm(pair_sources),
        in_hbm(body_cluster),
        *[in_hbm(a) for a in arrays],
    )


def far_rows(moments, picks, coupling, evaluation):
    groups = len(moments)
    blocks = 2 * groups
    width = evaluation.shape[1] // blocks
    sources, lags_here = coupling.shape[:2]
    terms = evaluation.shape[0]

    def body(picks_ref, coupling_ref, evaluation_ref, *rest):
        moments_refs, out_ref = rest[:groups], rest[groups]
        clus = lax.axis_index("clus")
        values = [ref[i].astype(F32) for ref in moments_refs for i in range(2)]
        values = jnp.concatenate(values, axis=0)
        wanted = jnp.dot(
            picks_ref[...].astype(jnp.bfloat16),
            values.astype(jnp.bfloat16),
            preferred_element_type=F32,
        )
        total = jnp.zeros(coupling_ref.shape[2:], F32)
        for k in range(sources):
            for j in range(lags_here):
                r = k * lags_here + j
                total += coupling_ref[k, j].astype(F32) * wanted[r : r + 1, :]
        local = jnp.sum(total, axis=1, keepdims=True)
        for t in range(blocks):
            start = pl.multiple_of((clus ^ t) * width, width)
            block = evaluation_ref[:, pl.ds(start, width)]
            out_ref[t : t + 1, :] = jnp.sum(block * local, axis=0, keepdims=True)

    return pl.pallas_call(
        body,
        out_shape=pltpu.VMEM((blocks, width), F32),
        in_specs=[VM] * (3 + groups),
        out_specs=VM,
        compiler_params=pltpu.CompilerParams(vmem_limit_bytes=LIMIT),
        cost_estimate=pl.CostEstimate(
            flops=2 * terms * evaluation.shape[1], bytes_accessed=3 << 20, transcendentals=0
        ),
        name="far_rows",
    )(in_vmem(picks), in_vmem(coupling), in_vmem(evaluation), *[in_vmem(v) for v in moments])


def partial_sums(pieces, kernel, far, mask):
    lag_count = len(pieces)
    lags_here, here, depth = pieces[0].shape
    rows = lag_count * here
    blocks, width = far.shape

    def body(mask_ref, far_ref, kernel_ref, *rest):
        keep_ref, send_ref = rest[lag_count], rest[lag_count + 1]
        pieces_ref = (rest[0],) + rest[lag_count - 1 : 0 : -1]
        clus = lax.axis_index("clus")
        mask = mask_ref[...]
        lhs = [
            jnp.concatenate([piece[j] for piece in pieces_ref], axis=0) for j in range(lags_here)
        ]
        for t in range(blocks):
            start = pl.multiple_of((clus ^ t) * width, width)
            total = mask * far_ref[t : t + 1, :]
            for j in range(lags_here):
                total += jnp.dot(
                    lhs[j], kernel_ref[j, :, pl.ds(start, width)], preferred_element_type=F32
                )
            out_ref = send_ref if t % 2 else keep_ref
            out_ref[t // 2] = total

    half = pltpu.VMEM((blocks // 2, rows, width), F32)
    return pl.pallas_call(
        body,
        out_shape=[half, half],
        in_specs=[VM] * (3 + lag_count),
        out_specs=[VM, VM],
        compiler_params=pltpu.CompilerParams(vmem_limit_bytes=LIMIT),
        cost_estimate=pl.CostEstimate(
            flops=2 * rows * lags_here * depth * kernel.shape[2],
            bytes_accessed=kernel.size * 2 + 4 * rows * width * blocks,
            transcendentals=0,
        ),
        name="partial_sums",
    )(in_vmem(mask), in_vmem(far), in_vmem(kernel), *[in_vmem(pieces[-s]) for s in range(lag_count)])


def shards(history, kernel, moments, coupling, evaluation, offsets, pair_sources, body_cluster):
    lag_count = lax.axis_size("lag")
    clus_count = lax.axis_size("clus")
    lags_here = kernel.shape[0]
    here = history.shape[1]

    beside = swap(moments[:, 0], "clus", 1)
    *pieces, mine = pick_slots(history, moments[:, 0], offsets, lag_count, lags_here)
    pieces = [pieces[0]] + [swap(pieces[s], "lag", s) for s in range(1, lag_count)]
    pair = jnp.stack([mine, beside])
    gathered = [pair] + [swap(pair, "clus", t) for t in range(2, clus_count, 2)]
    near, coupling_near, evaluation_near, mask, picks = bring_near(
        pair,
        [kernel, coupling[0], evaluation],
        offsets[None],
        pair_sources,
        body_cluster[None],
        here,
        lags_here,
    )
    far = far_rows(gathered, picks, coupling_near, evaluation_near)

    keep, send = partial_sums(pieces, near, far, mask)
    kept = [keep[i] for i in range(clus_count // 2)]
    came = swap(send, "clus", 1)
    kept = [kept[i] + came[i] for i in range(clus_count // 2)]
    bit = 2
    while bit < clus_count:
        came = [swap(value, "clus", bit) for value in kept[1::2]]
        kept = [a + b for a, b in zip(kept[0::2], came)]
        bit *= 2
    parts = [kept[0][s * here : (s + 1) * here] for s in range(lag_count)]
    owned = parts[0]
    for s in [lag_count - 1] + list(range(1, lag_count - 1)):
        owned = owned + swap(parts[s], "lag", s)
    return owned.astype(jnp.bfloat16)


def solution(mesh):
    in_specs = (
        P(None, ("farm", "lag"), "clus"),
        P("lag", "clus", None),
        P(None, ("farm", "clus"), None),
        P("clus", None, "lag", None, None),
        P(),
        P(),
        P(),
        P(),
    )
    out_specs = P(("farm", "lag"), "clus")
    return jax.shard_map(shards, mesh=mesh, in_specs=in_specs, out_specs=out_specs, check_vma=False)
```

```python
import jax
import jax.numpy as jnp
from jax import lax
from jax.experimental import pallas as pl
from jax.experimental.pallas import tpu as pltpu
from jax.sharding import PartitionSpec as P

F32 = jnp.float32
HBM = pl.BlockSpec(memory_space=pltpu.HBM)
VM = pl.BlockSpec(memory_space=pltpu.VMEM)
SM = pl.BlockSpec(memory_space=pltpu.SMEM)
LIMIT = 16 << 20


def swap(value, axis, bit):
    count = lax.axis_size(axis)
    return lax.ppermute(value, axis, [(i, i ^ bit) for i in range(count)])


def in_vmem(value):
    return pltpu.with_memory_space_constraint(value, pltpu.VMEM)


def in_hbm(value):
    return pltpu.with_memory_space_constraint(value, pltpu.HBM)


def exponents(value):
    top = jnp.max(jnp.abs(value), axis=0, keepdims=True)
    wanted = jnp.where(top > 0.0, jnp.ceil(jnp.log2(top)) - 14.0, 0.0)
    return jnp.clip(wanted, -120.0, 120.0)


def pack(value, exponent):
    rows = (value * jnp.exp2(-exponent)).astype(jnp.float16)
    last = jnp.broadcast_to(exponent, (8,) + rows.shape[1:]).astype(jnp.float16)
    return jnp.concatenate([rows, last], axis=0)


def unpack(message):
    return message[:-8].astype(F32) * jnp.exp2(message[-8:-7].astype(F32))


def pick_slots(history, moments, offsets, lag_count, lags_here):
    shape = (lags_here,) + history.shape[1:]

    def body(offsets_ref, history_ref, moments_ref, *rest):
        outs, moments_out = rest[:lag_count], rest[lag_count]
        sems, moments_sem = rest[lag_count + 1 :]
        me = lax.axis_index("lag")
        copies = [pltpu.make_async_copy(moments_ref, moments_out, moments_sem)]
        for s in range(lag_count):
            for j in range(lags_here):
                slot = offsets_ref[(me ^ s) * lags_here + j]
                copies.append(
                    pltpu.make_async_copy(history_ref.at[slot], outs[s].at[j], sems.at[s, j])
                )
        for copy in copies:
            copy.start()
        for copy in copies:
            copy.wait()

    return pl.pallas_call(
        body,
        out_shape=[pltpu.VMEM(shape, history.dtype)] * lag_count
        + [pltpu.VMEM(moments.shape, moments.dtype)],
        in_specs=[SM, HBM, HBM],
        out_specs=[VM] * (lag_count + 1),
        scratch_shapes=[
            pltpu.SemaphoreType.DMA((lag_count, lags_here)),
            pltpu.SemaphoreType.DMA,
        ],
        compiler_params=pltpu.CompilerParams(vmem_limit_bytes=LIMIT),
        name="pick_slots",
    )(in_hbm(offsets), in_hbm(history), in_hbm(moments))


def bring_near(arrived, arrays, offsets, pair_sources, body_cluster, here, lags_here):
    count = len(arrays)
    rows = body_cluster.shape[1]
    slots = offsets.shape[1]
    blocks, sources = pair_sources.shape

    def body(arrived_ref, offsets_hbm, pairs_hbm, clusters_hbm, *rest):
        sources_hbm, outs = rest[:count], rest[count : 2 * count]
        mask_ref, picks_ref, offsets_ref, pairs_ref, clusters_ref, sems = rest[2 * count :]
        copies = [
            pltpu.make_async_copy(offsets_hbm, offsets_ref, sems.at[0]),
            pltpu.make_async_copy(pairs_hbm, pairs_ref, sems.at[1]),
            pltpu.make_async_copy(clusters_hbm, clusters_ref, sems.at[2]),
        ]
        for i in range(count):
            copies.append(pltpu.make_async_copy(sources_hbm[i], outs[i], sems.at[3 + i]))
        for copy in copies:
            copy.start()
        for copy in copies[:3]:
            copy.wait()
        lag = lax.axis_index("lag")
        clus = lax.axis_index("clus")
        row = lax.broadcasted_iota(jnp.int32, (rows, rows), 0)
        column = lax.broadcasted_iota(jnp.int32, (rows, rows), 1)
        body_of_row = ((row // here) ^ lag) * here + row % here
        chosen = (column == body_of_row) & (clusters_ref[...] == clus)
        mask_ref[...] = jnp.sum(chosen.astype(F32), axis=1, keepdims=True)
        place = lax.broadcasted_iota(jnp.int32, (1, blocks * slots), 1)
        lag_at = lax.broadcasted_iota(jnp.int32, (1, slots), 1)
        pair_row = lax.broadcasted_iota(jnp.int32, (blocks, sources), 0)
        pair_at = lax.broadcasted_iota(jnp.int32, (blocks, sources), 1)
        offsets = offsets_ref[...]
        pairs = pairs_ref[...]
        for j in range(lags_here):
            slot = jnp.where(lag_at == lag * lags_here + j, offsets, 0)
            slot = jnp.sum(slot, axis=1, keepdims=True)
            for k in range(sources):
                source = jnp.where((pair_row == clus) & (pair_at == k), pairs, 0)
                source = jnp.sum(jnp.sum(source, axis=1, keepdims=True), axis=0, keepdims=True)
                at = (source ^ clus) * slots + slot
                r = k * lags_here + j
                picks_ref[r : r + 1, :] = (place == at).astype(F32)
        for copy in copies[3:]:
            copy.wait()

    return pl.pallas_call(
        body,
        out_shape=[pltpu.VMEM(a.shape, a.dtype) for a in arrays]
        + [pltpu.VMEM((rows, 1), F32), pltpu.VMEM((sources * lags_here, blocks * slots), F32)],
        in_specs=[VM] + [HBM] * (count + 3),
        out_specs=[VM] * (count + 2),
        scratch_shapes=[
            pltpu.VMEM(offsets.shape, jnp.int32),
            pltpu.VMEM(pair_sources.shape, jnp.int32),
            pltpu.VMEM(body_cluster.shape, jnp.int32),
            pltpu.SemaphoreType.DMA((count + 3,)),
        ],
        compiler_params=pltpu.CompilerParams(vmem_limit_bytes=LIMIT),
        cost_estimate=pl.CostEstimate(flops=0, bytes_accessed=7 << 20, transcendentals=0),
        name="bring_near",
    )(
        in_vmem(arrived),
        in_hbm(offsets),
        in_hbm(pair_sources),
        in_hbm(body_cluster),
        *[in_hbm(a) for a in arrays],
    )


def far_rows(moments, picks, coupling, evaluation):
    groups = len(moments)
    blocks = 2 * groups
    width = evaluation.shape[1] // blocks
    sources, lags_here = coupling.shape[:2]
    terms = evaluation.shape[0]

    def body(picks_ref, coupling_ref, evaluation_ref, *rest):
        moments_refs, out_ref = rest[:groups], rest[groups]
        clus = lax.axis_index("clus")
        values = [ref[i].astype(F32) for ref in moments_refs for i in range(2)]
        values = jnp.concatenate(values, axis=0)
        wanted = jnp.dot(
            picks_ref[...].astype(jnp.bfloat16),
            values.astype(jnp.bfloat16),
            preferred_element_type=F32,
        )
        total = jnp.zeros(coupling_ref.shape[2:], F32)
        for k in range(sources):
            for j in range(lags_here):
                r = k * lags_here + j
                total += coupling_ref[k, j].astype(F32) * wanted[r : r + 1, :]
        local = jnp.sum(total, axis=1, keepdims=True)
        for t in range(blocks):
            start = pl.multiple_of((clus ^ t) * width, width)
            block = evaluation_ref[:, pl.ds(start, width)]
            out_ref[t : t + 1, :] = jnp.sum(block * local, axis=0, keepdims=True)

    return pl.pallas_call(
        body,
        out_shape=pltpu.VMEM((blocks, width), F32),
        in_specs=[VM] * (3 + groups),
        out_specs=VM,
        compiler_params=pltpu.CompilerParams(vmem_limit_bytes=LIMIT),
        cost_estimate=pl.CostEstimate(
            flops=2 * terms * evaluation.shape[1], bytes_accessed=3 << 20, transcendentals=0
        ),
        name="far_rows",
    )(in_vmem(picks), in_vmem(coupling), in_vmem(evaluation), *[in_vmem(v) for v in moments])


def partial_sums(pieces, kernel, far, mask, odd):
    lag_count = len(pieces)
    lags_here, here, depth = pieces[0].shape
    rows = lag_count * here
    half = rows // 2
    blocks, width = far.shape
    count = blocks // 2

    def body(mask_ref, far_ref, kernel_ref, *rest):
        outs = rest[lag_count:]
        pieces_ref = (rest[0],) + rest[lag_count - 1 : 0 : -1]
        clus = lax.axis_index("clus")
        mask = mask_ref[...]
        lhs = [
            jnp.concatenate([piece[j] for piece in pieces_ref], axis=0) for j in range(lags_here)
        ]
        for i in range(count):
            t = 2 * i + odd
            start = pl.multiple_of((clus ^ t) * width, width)
            total = mask * far_ref[t : t + 1, :]
            for j in range(lags_here):
                total += jnp.dot(
                    lhs[j], kernel_ref[j, :, pl.ds(start, width)], preferred_element_type=F32
                )
            outs[0][i] = total[:half]
            outs[1][i] = total[half:]

    part = pltpu.VMEM((count, half, width), F32)
    return pl.pallas_call(
        body,
        out_shape=[part, part],
        in_specs=[VM] * (3 + lag_count),
        out_specs=[VM, VM],
        compiler_params=pltpu.CompilerParams(vmem_limit_bytes=LIMIT),
        cost_estimate=pl.CostEstimate(
            flops=rows * lags_here * depth * kernel.shape[2],
            bytes_accessed=kernel.size + 4 * rows * width * count,
            transcendentals=0,
        ),
        name=f"partial_sums_{odd}",
    )(in_vmem(mask), in_vmem(far), in_vmem(kernel), *[in_vmem(pieces[-s]) for s in range(lag_count)])


def shards(history, kernel, moments, coupling, evaluation, offsets, pair_sources, body_cluster):
    lag_count = lax.axis_size("lag")
    clus_count = lax.axis_size("clus")
    lags_here = kernel.shape[0]
    here = history.shape[1]

    beside = swap(moments[:, 0], "clus", 1)
    *pieces, mine = pick_slots(history, moments[:, 0], offsets, lag_count, lags_here)
    pieces = [pieces[0]] + [swap(pieces[s], "lag", s) for s in range(1, lag_count)]
    pair = jnp.stack([mine, beside])
    gathered = [pair] + [swap(pair, "clus", t) for t in range(2, clus_count, 2)]
    near, coupling_near, evaluation_near, mask, picks = bring_near(
        pair,
        [kernel, coupling[0], evaluation],
        offsets[None],
        pair_sources,
        body_cluster[None],
        here,
        lags_here,
    )
    far = far_rows(gathered, picks, coupling_near, evaluation_near)

    send = partial_sums(pieces, near, far, mask, 1)
    keep = partial_sums(pieces, near, far, mask, 0)
    middle = lag_count // 2
    sums = {}
    for h in (1, 0):
        total = keep[h] + swap(send[h], "clus", 1)
        kept = [total[i] for i in range(clus_count // 2)]
        bit = 2
        while bit < clus_count:
            came = [unpack(swap(pack(v, exponents(v)), "clus", bit)) for v in kept[1::2]]
            kept = [a + b for a, b in zip(kept[0::2], came)]
            bit *= 2
        sums[h] = kept[0]
    owned = None
    for s in range(lag_count - 1, -1, -1):
        h, at = s // middle, (s % middle) * here
        part = sums[h][at : at + here]
        if s > 0:
            part = swap(part, "lag", s)
        owned = part if owned is None else owned + part
    return owned.astype(jnp.bfloat16)


def solution(mesh):
    in_specs = (
        P(None, ("farm", "lag"), "clus"),
        P("lag", "clus", None),
        P(None, ("farm", "clus"), None),
        P("clus", None, "lag", None, None),
        P(),
        P(),
        P(),
        P(),
    )
    out_specs = P(("farm", "lag"), "clus")
    return jax.shard_map(shards, mesh=mesh, in_specs=in_specs, out_specs=out_specs, check_vma=False)
```

```python
import jax
import jax.numpy as jnp
from jax import lax
from jax.experimental import pallas as pl
from jax.experimental.pallas import tpu as pltpu
from jax.sharding import PartitionSpec as P

F32 = jnp.float32
HBM = pl.BlockSpec(memory_space=pltpu.HBM)
VM = pl.BlockSpec(memory_space=pltpu.VMEM)
SM = pl.BlockSpec(memory_space=pltpu.SMEM)
LIMIT = 16 << 20


def swap(value, axis, bit):
    count = lax.axis_size(axis)
    return lax.ppermute(value, axis, [(i, i ^ bit) for i in range(count)])


def in_vmem(value):
    return pltpu.with_memory_space_constraint(value, pltpu.VMEM)


def in_hbm(value):
    return pltpu.with_memory_space_constraint(value, pltpu.HBM)


def exponents(value):
    top = jnp.max(jnp.abs(value), axis=0, keepdims=True)
    wanted = jnp.where(top > 0.0, jnp.ceil(jnp.log2(top)) - 14.0, 0.0)
    return jnp.clip(wanted, -120.0, 120.0)


def pack(value, exponent):
    rows = (value * jnp.exp2(-exponent)).astype(jnp.float16)
    last = jnp.broadcast_to(exponent, (8,) + rows.shape[1:]).astype(jnp.float16)
    return jnp.concatenate([rows, last], axis=0)


def unpack(message):
    return message[:-8].astype(F32) * jnp.exp2(message[-8:-7].astype(F32))


def pick_slots(history, moments, offsets, arrays, lag_count, lags_here):
    shape = (lags_here,) + history.shape[1:]
    count = len(arrays)

    def body(offsets_hbm, history_ref, moments_ref, *rest):
        arrays_hbm, rest = rest[:count], rest[count:]
        outs, moments_out = rest[:lag_count], rest[lag_count]
        arrays_out, rest = rest[lag_count + 1 : lag_count + 1 + count], rest[lag_count + 1 + count :]
        offsets_ref, sems, other_sems = rest
        me = lax.axis_index("lag")
        first = pltpu.make_async_copy(offsets_hbm, offsets_ref, other_sems.at[0])
        first.start()
        copies = [pltpu.make_async_copy(moments_ref, moments_out, other_sems.at[1])]
        for i in range(count):
            copies.append(
                pltpu.make_async_copy(arrays_hbm[i], arrays_out[i], other_sems.at[2 + i])
            )
        for copy in copies:
            copy.start()
        first.wait()
        slots = []
        for s in range(lag_count):
            for j in range(lags_here):
                slot = offsets_ref[(me ^ s) * lags_here + j]
                slots.append(
                    pltpu.make_async_copy(history_ref.at[slot], outs[s].at[j], sems.at[s, j])
                )
        for copy in slots:
            copy.start()
        for copy in copies + slots:
            copy.wait()

    return pl.pallas_call(
        body,
        out_shape=[pltpu.VMEM(shape, history.dtype)] * lag_count
        + [pltpu.VMEM(a.shape, a.dtype) for a in [moments] + arrays],
        in_specs=[HBM] * (3 + count),
        out_specs=[VM] * (lag_count + 1 + count),
        scratch_shapes=[
            pltpu.SMEM(offsets.shape, jnp.int32),
            pltpu.SemaphoreType.DMA((lag_count, lags_here)),
            pltpu.SemaphoreType.DMA((2 + count,)),
        ],
        compiler_params=pltpu.CompilerParams(vmem_limit_bytes=LIMIT),
        name="pick_slots",
    )(in_hbm(offsets), in_hbm(history), in_hbm(moments), *[in_hbm(a) for a in arrays])


def bring_near(arrived, arrays, offsets, pair_sources, body_cluster, here, lags_here):
    count = len(arrays)
    rows = body_cluster.shape[1]
    slots = offsets.shape[1]
    blocks, sources = pair_sources.shape

    def body(arrived_ref, offsets_hbm, pairs_hbm, clusters_hbm, *rest):
        sources_hbm, outs = rest[:count], rest[count : 2 * count]
        mask_ref, picks_ref, offsets_ref, pairs_ref, clusters_ref, sems = rest[2 * count :]
        copies = [
            pltpu.make_async_copy(offsets_hbm, offsets_ref, sems.at[0]),
            pltpu.make_async_copy(pairs_hbm, pairs_ref, sems.at[1]),
            pltpu.make_async_copy(clusters_hbm, clusters_ref, sems.at[2]),
        ]
        for i in range(count):
            copies.append(pltpu.make_async_copy(sources_hbm[i], outs[i], sems.at[3 + i]))
        for copy in copies:
            copy.start()
        for copy in copies[:3]:
            copy.wait()
        lag = lax.axis_index("lag")
        clus = lax.axis_index("clus")
        row = lax.broadcasted_iota(jnp.int32, (rows, rows), 0)
        column = lax.broadcasted_iota(jnp.int32, (rows, rows), 1)
        body_of_row = ((row // here) ^ lag) * here + row % here
        chosen = (column == body_of_row) & (clusters_ref[...] == clus)
        mask_ref[...] = jnp.sum(chosen.astype(F32), axis=1, keepdims=True)
        place = lax.broadcasted_iota(jnp.int32, (1, blocks * slots), 1)
        lag_at = lax.broadcasted_iota(jnp.int32, (1, slots), 1)
        pair_row = lax.broadcasted_iota(jnp.int32, (blocks, sources), 0)
        pair_at = lax.broadcasted_iota(jnp.int32, (blocks, sources), 1)
        offsets = offsets_ref[...]
        pairs = pairs_ref[...]
        for j in range(lags_here):
            slot = jnp.where(lag_at == lag * lags_here + j, offsets, 0)
            slot = jnp.sum(slot, axis=1, keepdims=True)
            for k in range(sources):
                source = jnp.where((pair_row == clus) & (pair_at == k), pairs, 0)
                source = jnp.sum(jnp.sum(source, axis=1, keepdims=True), axis=0, keepdims=True)
                at = (source ^ clus) * slots + slot
                r = k * lags_here + j
                picks_ref[r : r + 1, :] = (place == at).astype(F32)
        for copy in copies[3:]:
            copy.wait()

    return pl.pallas_call(
        body,
        out_shape=[pltpu.VMEM(a.shape, a.dtype) for a in arrays]
        + [pltpu.VMEM((rows, 1), F32), pltpu.VMEM((sources * lags_here, blocks * slots), F32)],
        in_specs=[VM] + [HBM] * (count + 3),
        out_specs=[VM] * (count + 2),
        scratch_shapes=[
            pltpu.VMEM(offsets.shape, jnp.int32),
            pltpu.VMEM(pair_sources.shape, jnp.int32),
            pltpu.VMEM(body_cluster.shape, jnp.int32),
            pltpu.SemaphoreType.DMA((count + 3,)),
        ],
        compiler_params=pltpu.CompilerParams(vmem_limit_bytes=LIMIT),
        cost_estimate=pl.CostEstimate(flops=0, bytes_accessed=7 << 20, transcendentals=0),
        name="bring_near",
    )(
        in_vmem(arrived),
        in_hbm(offsets),
        in_hbm(pair_sources),
        in_hbm(body_cluster),
        *[in_hbm(a) for a in arrays],
    )


def far_rows(moments, picks, coupling, evaluation):
    groups = len(moments)
    blocks = 2 * groups
    width = evaluation.shape[1] // blocks
    sources, lags_here = coupling.shape[:2]
    terms = evaluation.shape[0]

    def body(picks_ref, coupling_ref, evaluation_ref, *rest):
        moments_refs, out_ref = rest[:groups], rest[groups]
        clus = lax.axis_index("clus")
        values = [ref[i].astype(F32) for ref in moments_refs for i in range(2)]
        values = jnp.concatenate(values, axis=0)
        wanted = jnp.dot(
            picks_ref[...].astype(jnp.bfloat16),
            values.astype(jnp.bfloat16),
            preferred_element_type=F32,
        )
        total = jnp.zeros(coupling_ref.shape[2:], F32)
        for k in range(sources):
            for j in range(lags_here):
                r = k * lags_here + j
                total += coupling_ref[k, j].astype(F32) * wanted[r : r + 1, :]
        local = jnp.sum(total, axis=1, keepdims=True)
        for t in range(blocks):
            start = pl.multiple_of((clus ^ t) * width, width)
            block = evaluation_ref[:, pl.ds(start, width)]
            out_ref[t : t + 1, :] = jnp.sum(block * local, axis=0, keepdims=True)

    return pl.pallas_call(
        body,
        out_shape=pltpu.VMEM((blocks, width), F32),
        in_specs=[VM] * (3 + groups),
        out_specs=VM,
        compiler_params=pltpu.CompilerParams(vmem_limit_bytes=LIMIT),
        cost_estimate=pl.CostEstimate(
            flops=2 * terms * evaluation.shape[1], bytes_accessed=3 << 20, transcendentals=0
        ),
        name="far_rows",
    )(in_vmem(picks), in_vmem(coupling), in_vmem(evaluation), *[in_vmem(v) for v in moments])


def partial_sums(pieces, kernel, far, mask, odd):
    lag_count = len(pieces)
    lags_here, here, depth = pieces[0].shape
    rows = lag_count * here
    half = rows // 2
    blocks, width = far.shape
    count = blocks // 2

    def body(mask_ref, far_ref, kernel_ref, *rest):
        outs = rest[lag_count:]
        pieces_ref = (rest[0],) + rest[lag_count - 1 : 0 : -1]
        clus = lax.axis_index("clus")
        mask = mask_ref[...]
        lhs = [
            jnp.concatenate([piece[j] for piece in pieces_ref], axis=0) for j in range(lags_here)
        ]
        for i in range(count):
            t = 2 * i + odd
            start = pl.multiple_of((clus ^ t) * width, width)
            total = mask * far_ref[t : t + 1, :]
            for j in range(lags_here):
                total += jnp.dot(
                    lhs[j], kernel_ref[j, :, pl.ds(start, width)], preferred_element_type=F32
                )
            outs[0][i] = total[:half]
            outs[1][i] = total[half:]

    part = pltpu.VMEM((count, half, width), F32)
    return pl.pallas_call(
        body,
        out_shape=[part, part],
        in_specs=[VM] * (3 + lag_count),
        out_specs=[VM, VM],
        compiler_params=pltpu.CompilerParams(vmem_limit_bytes=LIMIT),
        cost_estimate=pl.CostEstimate(
            flops=rows * lags_here * depth * kernel.shape[2],
            bytes_accessed=kernel.size + 4 * rows * width * count,
            transcendentals=0,
        ),
        name=f"partial_sums_{odd}",
    )(in_vmem(mask), in_vmem(far), in_vmem(kernel), *[in_vmem(pieces[-s]) for s in range(lag_count)])


def shards(history, kernel, moments, coupling, evaluation, offsets, pair_sources, body_cluster):
    lag_count = lax.axis_size("lag")
    clus_count = lax.axis_size("clus")
    lags_here = kernel.shape[0]
    here = history.shape[1]

    beside = swap(moments[:, 0], "clus", 1)
    *pieces, mine, coupling_near, evaluation_near = pick_slots(
        history, moments[:, 0], offsets, [coupling[0], evaluation], lag_count, lags_here
    )
    pieces = [pieces[0]] + [swap(pieces[s], "lag", s) for s in range(1, lag_count)]
    pair = jnp.stack([mine, beside])
    gathered = [pair] + [swap(pair, "clus", t) for t in range(2, clus_count, 2)]
    near, mask, picks = bring_near(
        pair,
        [kernel],
        offsets[None],
        pair_sources,
        body_cluster[None],
        here,
        lags_here,
    )
    far = far_rows(gathered, picks, coupling_near, evaluation_near)

    send = partial_sums(pieces, near, far, mask, 1)
    keep = partial_sums(pieces, near, far, mask, 0)
    middle = lag_count // 2
    sums = {}
    for h in (1, 0):
        total = keep[h] + swap(send[h], "clus", 1)
        kept = [total[i] for i in range(clus_count // 2)]
        bit = 2
        while bit < clus_count:
            came = [unpack(swap(pack(v, exponents(v)), "clus", bit)) for v in kept[1::2]]
            kept = [a + b for a, b in zip(kept[0::2], came)]
            bit *= 2
        sums[h] = kept[0]
    owned = None
    for s in range(lag_count - 1, -1, -1):
        h, at = s // middle, (s % middle) * here
        part = sums[h][at : at + here]
        if s > 0:
            part = swap(part, "lag", s)
        owned = part if owned is None else owned + part
    return owned.astype(jnp.bfloat16)


def solution(mesh):
    in_specs = (
        P(None, ("farm", "lag"), "clus"),
        P("lag", "clus", None),
        P(None, ("farm", "clus"), None),
        P("clus", None, "lag", None, None),
        P(),
        P(),
        P(),
        P(),
    )
    out_specs = P(("farm", "lag"), "clus")
    return jax.shard_map(shards, mesh=mesh, in_specs=in_specs, out_specs=out_specs, check_vma=False)
```

```python
import jax
import jax.numpy as jnp
from jax import lax
from jax.experimental import pallas as pl
from jax.experimental.pallas import tpu as pltpu
from jax.sharding import PartitionSpec as P

F32 = jnp.float32
HBM = pl.BlockSpec(memory_space=pltpu.HBM)
VM = pl.BlockSpec(memory_space=pltpu.VMEM)
SM = pl.BlockSpec(memory_space=pltpu.SMEM)
LIMIT = 16 << 20
CUTS = 2


def swap(value, axis, bit):
    count = lax.axis_size(axis)
    return lax.ppermute(value, axis, [(i, i ^ bit) for i in range(count)])


def turn(value, axis, step):
    count = lax.axis_size(axis)
    return lax.ppermute(value, axis, [(i, (i + step) % count) for i in range(count)])


def in_vmem(value):
    return pltpu.with_memory_space_constraint(value, pltpu.VMEM)


def in_hbm(value):
    return pltpu.with_memory_space_constraint(value, pltpu.HBM)


def exponents(value):
    top = jnp.max(jnp.abs(value), axis=0, keepdims=True)
    wanted = jnp.where(top > 0.0, jnp.ceil(jnp.log2(top)) - 14.0, 0.0)
    return jnp.clip(wanted, -120.0, 120.0)


def pack(value, exponent):
    rows = (value * jnp.exp2(-exponent)).astype(jnp.float16)
    last = jnp.broadcast_to(exponent, (8,) + rows.shape[1:]).astype(jnp.float16)
    return jnp.concatenate([rows, last], axis=0)


def unpack(message):
    return message[:-8].astype(F32) * jnp.exp2(message[-8:-7].astype(F32))


def pick_slots(history, moments, offsets, pair_sources, body_cluster, arrays, lag_count, lags_here):
    here = history.shape[1]
    shape = (lags_here,) + history.shape[1:]
    count = len(arrays)
    rows = body_cluster.shape[1]
    slots = offsets.shape[0]
    blocks, sources = pair_sources.shape

    def body(offsets_hbm, pairs_hbm, clusters_hbm, history_ref, moments_ref, *rest):
        arrays_hbm, rest = rest[:count], rest[count:]
        outs, rest = rest[:lag_count], rest[lag_count:]
        moments_out, mask_ref, picks_ref = rest[:3]
        arrays_out, rest = rest[3 : 3 + count], rest[3 + count :]
        offsets_ref, pairs_ref, clusters_ref, sems, other_sems = rest
        lag = lax.axis_index("lag")
        clus = lax.axis_index("clus")
        small = [
            pltpu.make_async_copy(offsets_hbm, offsets_ref, other_sems.at[0]),
            pltpu.make_async_copy(pairs_hbm, pairs_ref, other_sems.at[1]),
            pltpu.make_async_copy(clusters_hbm, clusters_ref, other_sems.at[2]),
        ]
        copies = [pltpu.make_async_copy(moments_ref, moments_out, other_sems.at[3])]
        for i in range(count):
            copies.append(
                pltpu.make_async_copy(arrays_hbm[i], arrays_out[i], other_sems.at[4 + i])
            )
        for copy in small + copies:
            copy.start()
        small[0].wait()
        for s in range(lag_count):
            for j in range(lags_here):
                slot = offsets_ref[lax.rem(lag + s, lag_count) * lags_here + j]
                copies.append(
                    pltpu.make_async_copy(history_ref.at[slot], outs[s].at[j], sems.at[s, j])
                )
                copies[-1].start()
        small[1].wait()
        place = lax.broadcasted_iota(jnp.int32, (1, blocks * slots), 1)
        for j in range(lags_here):
            slot = offsets_ref[lag * lags_here + j]
            for k in range(sources):
                at = (pairs_ref[clus, k] ^ clus) * slots + slot
                r = k * lags_here + j
                picks_ref[r : r + 1, :] = (place == at).astype(F32)
        small[2].wait()
        row = lax.broadcasted_iota(jnp.int32, (rows, rows), 0)
        column = lax.broadcasted_iota(jnp.int32, (rows, rows), 1)
        body_of_row = lax.rem(lag + lag_count - row // here, lag_count) * here + row % here
        chosen = (column == body_of_row) & (clusters_ref[...] == clus)
        mask_ref[...] = jnp.sum(chosen.astype(F32), axis=1, keepdims=True)
        for copy in copies:
            copy.wait()

    return pl.pallas_call(
        body,
        out_shape=[pltpu.VMEM(shape, history.dtype)] * lag_count
        + [
            pltpu.VMEM(moments.shape, moments.dtype),
            pltpu.VMEM((rows, 1), F32),
            pltpu.VMEM((sources * lags_here, blocks * slots), F32),
        ]
        + [pltpu.VMEM(a.shape, a.dtype) for a in arrays],
        in_specs=[HBM] * (5 + count),
        out_specs=[VM] * (lag_count + 3 + count),
        scratch_shapes=[
            pltpu.SMEM(offsets.shape, jnp.int32),
            pltpu.SMEM(pair_sources.shape, jnp.int32),
            pltpu.VMEM(body_cluster.shape, jnp.int32),
            pltpu.SemaphoreType.DMA((lag_count, lags_here)),
            pltpu.SemaphoreType.DMA((4 + count,)),
        ],
        compiler_params=pltpu.CompilerParams(vmem_limit_bytes=LIMIT),
        name="pick_slots",
    )(
        in_hbm(offsets),
        in_hbm(pair_sources),
        in_hbm(body_cluster),
        in_hbm(history),
        in_hbm(moments),
        *[in_hbm(a) for a in arrays],
    )


def bring_near(arrived, array):
    def body(arrived_ref, array_hbm, out_ref, sem):
        part = array.shape[1] // CUTS
        copies = []
        for i in range(array.shape[0]):
            for c in range(CUTS):
                at = (i, pl.ds(c * part, part))
                copies.append(
                    pltpu.make_async_copy(array_hbm.at[at], out_ref.at[at], sem.at[i, c])
                )
        for copy in copies:
            copy.start()
        for copy in copies:
            copy.wait()

    return pl.pallas_call(
        body,
        out_shape=pltpu.VMEM(array.shape, array.dtype),
        in_specs=[VM, HBM],
        out_specs=VM,
        scratch_shapes=[pltpu.SemaphoreType.DMA((array.shape[0], CUTS))],
        compiler_params=pltpu.CompilerParams(vmem_limit_bytes=LIMIT),
        cost_estimate=pl.CostEstimate(
            flops=0, bytes_accessed=2 * array.size * array.dtype.itemsize, transcendentals=0
        ),
        name="bring_near",
    )(in_vmem(arrived), in_hbm(array))


def far_rows(moments, picks, coupling, evaluation):
    groups = len(moments)
    blocks = 2 * groups
    width = evaluation.shape[1] // blocks
    sources, lags_here = coupling.shape[:2]
    terms = evaluation.shape[0]

    def body(picks_ref, coupling_ref, evaluation_ref, *rest):
        moments_refs, out_ref = rest[:groups], rest[groups]
        clus = lax.axis_index("clus")
        values = [ref[i].astype(F32) for ref in moments_refs for i in range(2)]
        values = jnp.concatenate(values, axis=0)
        wanted = jnp.dot(
            picks_ref[...].astype(jnp.bfloat16),
            values.astype(jnp.bfloat16),
            preferred_element_type=F32,
        )
        total = jnp.zeros(coupling_ref.shape[2:], F32)
        for k in range(sources):
            for j in range(lags_here):
                r = k * lags_here + j
                total += coupling_ref[k, j].astype(F32) * wanted[r : r + 1, :]
        local = jnp.sum(total, axis=1, keepdims=True)
        for t in range(blocks):
            start = pl.multiple_of((clus ^ t) * width, width)
            block = evaluation_ref[:, pl.ds(start, width)]
            out_ref[t : t + 1, :] = jnp.sum(block * local, axis=0, keepdims=True)

    return pl.pallas_call(
        body,
        out_shape=pltpu.VMEM((blocks, width), F32),
        in_specs=[VM] * (3 + groups),
        out_specs=VM,
        compiler_params=pltpu.CompilerParams(vmem_limit_bytes=LIMIT),
        cost_estimate=pl.CostEstimate(
            flops=2 * terms * evaluation.shape[1], bytes_accessed=3 << 20, transcendentals=0
        ),
        name="far_rows",
    )(in_vmem(picks), in_vmem(coupling), in_vmem(evaluation), *[in_vmem(v) for v in moments])


def partial_sums(pieces, kernel, far, mask, odd):
    lag_count = len(pieces)
    lags_here, here, depth = pieces[0].shape
    rows = lag_count * here
    half = rows // 2
    blocks, width = far.shape
    count = blocks // 2

    def body(mask_ref, far_ref, kernel_ref, *rest):
        outs = rest[lag_count:]
        pieces_ref = rest[:lag_count]
        clus = lax.axis_index("clus")
        mask = mask_ref[...]
        lhs = [
            jnp.concatenate([piece[j] for piece in pieces_ref], axis=0) for j in range(lags_here)
        ]
        for i in range(count):
            t = 2 * i + odd
            start = pl.multiple_of((clus ^ t) * width, width)
            total = mask * far_ref[t : t + 1, :]
            for j in range(lags_here):
                total += jnp.dot(
                    lhs[j], kernel_ref[j, :, pl.ds(start, width)], preferred_element_type=F32
                )
            outs[0][i] = total[:half]
            outs[1][i] = total[half:]

    part = pltpu.VMEM((count, half, width), F32)
    return pl.pallas_call(
        body,
        out_shape=[part, part],
        in_specs=[VM] * (3 + lag_count),
        out_specs=[VM, VM],
        compiler_params=pltpu.CompilerParams(vmem_limit_bytes=LIMIT),
        cost_estimate=pl.CostEstimate(
            flops=rows * lags_here * depth * kernel.shape[2],
            bytes_accessed=kernel.size + 4 * rows * width * count,
            transcendentals=0,
        ),
        name=f"partial_sums_{odd}",
    )(in_vmem(mask), in_vmem(far), in_vmem(kernel), *[in_vmem(piece) for piece in pieces])


def shards(history, kernel, moments, coupling, evaluation, offsets, pair_sources, body_cluster):
    lag_count = lax.axis_size("lag")
    clus_count = lax.axis_size("clus")
    lags_here = kernel.shape[0]
    here = history.shape[1]

    beside = swap(moments[:, 0], "clus", 1)
    *pieces, mine, mask, picks, coupling_near, evaluation_near = pick_slots(
        history,
        moments[:, 0],
        offsets,
        pair_sources,
        body_cluster[None],
        [coupling[0], evaluation],
        lag_count,
        lags_here,
    )
    pieces = [pieces[0]] + [turn(pieces[s], "lag", s) for s in range(1, lag_count)]
    pair = jnp.stack([mine, beside])
    gathered = [pair] + [swap(pair, "clus", t) for t in range(2, clus_count, 2)]
    near = bring_near(pair, kernel)
    far = far_rows(gathered, picks, coupling_near, evaluation_near)

    send = partial_sums(pieces, near, far, mask, 1)
    keep = partial_sums(pieces, near, far, mask, 0)
    middle = lag_count // 2
    sums = {}
    for h in (1, 0):
        total = keep[h] + swap(send[h], "clus", 1)
        kept = [total[i] for i in range(clus_count // 2)]
        bit = 2
        while bit < clus_count:
            came = [unpack(swap(pack(v, exponents(v)), "clus", bit)) for v in kept[1::2]]
            kept = [a + b for a, b in zip(kept[0::2], came)]
            bit *= 2
        sums[h] = kept[0]
    owned = None
    for s in range(lag_count - 1, -1, -1):
        h, at = s // middle, (s % middle) * here
        part = sums[h][at : at + here]
        if s > 0:
            part = turn(part, "lag", -s)
        owned = part if owned is None else owned + part
    return owned.astype(jnp.bfloat16)


def solution(mesh):
    in_specs = (
        P(None, ("farm", "lag"), "clus"),
        P("lag", "clus", None),
        P(None, ("farm", "clus"), None),
        P("clus", None, "lag", None, None),
        P(),
        P(),
        P(),
        P(),
    )
    out_specs = P(("farm", "lag"), "clus")
    return jax.shard_map(shards, mesh=mesh, in_specs=in_specs, out_specs=out_specs, check_vma=False)
```

```python
import jax
import jax.numpy as jnp
from jax import lax
from jax.experimental import pallas as pl
from jax.experimental.pallas import tpu as pltpu
from jax.sharding import PartitionSpec as P

F32 = jnp.float32
HBM = pl.BlockSpec(memory_space=pltpu.HBM)
VM = pl.BlockSpec(memory_space=pltpu.VMEM)
SM = pl.BlockSpec(memory_space=pltpu.SMEM)
LIMIT = 16 << 20
CUTS = 2


def swap(value, axis, bit):
    count = lax.axis_size(axis)
    return lax.ppermute(value, axis, [(i, i ^ bit) for i in range(count)])


def turn(value, axis, step):
    count = lax.axis_size(axis)
    return lax.ppermute(value, axis, [(i, (i + step) % count) for i in range(count)])


def in_vmem(value):
    return pltpu.with_memory_space_constraint(value, pltpu.VMEM)


def in_hbm(value):
    return pltpu.with_memory_space_constraint(value, pltpu.HBM)


def exponents(value):
    top = jnp.max(jnp.abs(value), axis=0, keepdims=True)
    wanted = jnp.where(top > 0.0, jnp.ceil(jnp.log2(top)) - 14.0, 0.0)
    return jnp.clip(wanted, -120.0, 120.0)


def pack(value, exponent):
    rows = (value * jnp.exp2(-exponent)).astype(jnp.float16)
    last = jnp.broadcast_to(exponent, (8,) + rows.shape[1:]).astype(jnp.float16)
    return jnp.concatenate([rows, last], axis=0)


def unpack(message):
    return message[:-8].astype(F32) * jnp.exp2(message[-8:-7].astype(F32))


def pick_slots(history, moments, offsets, pair_sources, body_cluster, arrays, lag_count, lags_here):
    here = history.shape[1]
    shape = (lags_here,) + history.shape[1:]
    count = len(arrays)
    rows = body_cluster.shape[1]
    slots = offsets.shape[0]
    blocks, sources = pair_sources.shape

    def body(offsets_hbm, pairs_hbm, clusters_hbm, history_ref, moments_ref, *rest):
        arrays_hbm, rest = rest[:count], rest[count:]
        outs, rest = rest[:lag_count], rest[lag_count:]
        moments_out, mask_ref, picks_ref = rest[:3]
        arrays_out, rest = rest[3 : 3 + count], rest[3 + count :]
        offsets_ref, pairs_ref, clusters_ref, sems, other_sems = rest
        lag = lax.axis_index("lag")
        clus = lax.axis_index("clus")
        small = [
            pltpu.make_async_copy(offsets_hbm, offsets_ref, other_sems.at[0]),
            pltpu.make_async_copy(pairs_hbm, pairs_ref, other_sems.at[1]),
            pltpu.make_async_copy(clusters_hbm, clusters_ref, other_sems.at[2]),
        ]
        copies = [pltpu.make_async_copy(moments_ref, moments_out, other_sems.at[3])]
        for i in range(count):
            copies.append(
                pltpu.make_async_copy(arrays_hbm[i], arrays_out[i], other_sems.at[4 + i])
            )
        for copy in small + copies:
            copy.start()
        small[0].wait()
        for s in range(lag_count):
            for j in range(lags_here):
                slot = offsets_ref[lax.rem(lag + s, lag_count) * lags_here + j]
                copies.append(
                    pltpu.make_async_copy(history_ref.at[slot], outs[s].at[j], sems.at[s, j])
                )
                copies[-1].start()
        small[1].wait()
        place = lax.broadcasted_iota(jnp.int32, (1, blocks * slots), 1)
        for j in range(lags_here):
            slot = offsets_ref[lag * lags_here + j]
            for k in range(sources):
                at = (pairs_ref[clus, k] ^ clus) * slots + slot
                r = k * lags_here + j
                picks_ref[r : r + 1, :] = (place == at).astype(F32)
        small[2].wait()
        row = lax.broadcasted_iota(jnp.int32, (rows, rows), 0)
        column = lax.broadcasted_iota(jnp.int32, (rows, rows), 1)
        body_of_row = lax.rem(lag + lag_count - row // here, lag_count) * here + row % here
        chosen = (column == body_of_row) & (clusters_ref[...] == clus)
        mask_ref[...] = jnp.sum(chosen.astype(F32), axis=1, keepdims=True)
        for copy in copies:
            copy.wait()

    return pl.pallas_call(
        body,
        out_shape=[pltpu.VMEM(shape, history.dtype)] * lag_count
        + [
            pltpu.VMEM(moments.shape, moments.dtype),
            pltpu.VMEM((rows, 1), F32),
            pltpu.VMEM((sources * lags_here, blocks * slots), F32),
        ]
        + [pltpu.VMEM(a.shape, a.dtype) for a in arrays],
        in_specs=[HBM] * (5 + count),
        out_specs=[VM] * (lag_count + 3 + count),
        scratch_shapes=[
            pltpu.SMEM(offsets.shape, jnp.int32),
            pltpu.SMEM(pair_sources.shape, jnp.int32),
            pltpu.VMEM(body_cluster.shape, jnp.int32),
            pltpu.SemaphoreType.DMA((lag_count, lags_here)),
            pltpu.SemaphoreType.DMA((4 + count,)),
        ],
        compiler_params=pltpu.CompilerParams(vmem_limit_bytes=LIMIT),
        name="pick_slots",
    )(
        in_hbm(offsets),
        in_hbm(pair_sources),
        in_hbm(body_cluster),
        in_hbm(history),
        in_hbm(moments),
        *[in_hbm(a) for a in arrays],
    )


def bring_near(arrived, array):
    def body(arrived_ref, array_hbm, out_ref, sem):
        part = array.shape[1] // CUTS
        copies = []
        for i in range(array.shape[0]):
            for c in range(CUTS):
                at = (i, pl.ds(c * part, part))
                copies.append(
                    pltpu.make_async_copy(array_hbm.at[at], out_ref.at[at], sem.at[i, c])
                )
        for copy in copies:
            copy.start()
        for copy in copies:
            copy.wait()

    return pl.pallas_call(
        body,
        out_shape=pltpu.VMEM(array.shape, array.dtype),
        in_specs=[VM, HBM],
        out_specs=VM,
        scratch_shapes=[pltpu.SemaphoreType.DMA((array.shape[0], CUTS))],
        compiler_params=pltpu.CompilerParams(vmem_limit_bytes=LIMIT),
        cost_estimate=pl.CostEstimate(
            flops=0, bytes_accessed=2 * array.size * array.dtype.itemsize, transcendentals=0
        ),
        name="bring_near",
    )(in_vmem(arrived), in_hbm(array))


def far_rows(moments, picks, coupling, evaluation):
    groups = len(moments)
    blocks = 2 * groups
    width = evaluation.shape[1] // blocks
    sources, lags_here = coupling.shape[:2]
    terms = evaluation.shape[0]

    def body(picks_ref, coupling_ref, evaluation_ref, *rest):
        moments_refs, out_ref = rest[:groups], rest[groups]
        clus = lax.axis_index("clus")
        values = [ref[i].astype(F32) for ref in moments_refs for i in range(2)]
        values = jnp.concatenate(values, axis=0)
        wanted = jnp.dot(
            picks_ref[...].astype(jnp.bfloat16),
            values.astype(jnp.bfloat16),
            preferred_element_type=F32,
        )
        total = jnp.zeros(coupling_ref.shape[2:], F32)
        for k in range(sources):
            for j in range(lags_here):
                r = k * lags_here + j
                total += coupling_ref[k, j].astype(F32) * wanted[r : r + 1, :]
        local = jnp.sum(total, axis=1, keepdims=True)
        for t in range(blocks):
            start = pl.multiple_of((clus ^ t) * width, width)
            block = evaluation_ref[:, pl.ds(start, width)]
            out_ref[t : t + 1, :] = jnp.sum(block * local, axis=0, keepdims=True)

    return pl.pallas_call(
        body,
        out_shape=pltpu.VMEM((blocks, width), F32),
        in_specs=[VM] * (3 + groups),
        out_specs=VM,
        compiler_params=pltpu.CompilerParams(vmem_limit_bytes=LIMIT),
        cost_estimate=pl.CostEstimate(
            flops=2 * terms * evaluation.shape[1], bytes_accessed=3 << 20, transcendentals=0
        ),
        name="far_rows",
    )(in_vmem(picks), in_vmem(coupling), in_vmem(evaluation), *[in_vmem(v) for v in moments])


def partial_sums(pieces, kernel, far, mask, odd):
    lag_count = len(pieces)
    lags_here, here, depth = pieces[0].shape
    rows = lag_count * here
    half = rows // 2
    blocks, width = far.shape
    count = blocks // 2

    def body(mask_ref, far_ref, kernel_ref, *rest):
        outs = rest[lag_count:]
        pieces_ref = rest[:lag_count]
        clus = lax.axis_index("clus")
        mask = mask_ref[...]
        lhs = [
            jnp.concatenate([piece[j] for piece in pieces_ref], axis=0) for j in range(lags_here)
        ]
        for i in range(count):
            t = 2 * i + odd
            start = pl.multiple_of((clus ^ t) * width, width)
            total = mask * far_ref[t : t + 1, :]
            for j in range(lags_here):
                total += jnp.dot(
                    lhs[j], kernel_ref[j, :, pl.ds(start, width)], preferred_element_type=F32
                )
            outs[0][i] = total[:half]
            outs[1][i] = total[half:]

    part = pltpu.VMEM((count, half, width), F32)
    return pl.pallas_call(
        body,
        out_shape=[part, part],
        in_specs=[VM] * (3 + lag_count),
        out_specs=[VM, VM],
        compiler_params=pltpu.CompilerParams(vmem_limit_bytes=LIMIT),
        cost_estimate=pl.CostEstimate(
            flops=rows * lags_here * depth * kernel.shape[2],
            bytes_accessed=kernel.size + 4 * rows * width * count,
            transcendentals=0,
        ),
        name=f"partial_sums_{odd}",
    )(in_vmem(mask), in_vmem(far), in_vmem(kernel), *[in_vmem(piece) for piece in pieces])


def shards(history, kernel, moments, coupling, evaluation, offsets, pair_sources, body_cluster):
    lag_count = lax.axis_size("lag")
    clus_count = lax.axis_size("clus")
    lags_here = kernel.shape[0]
    here = history.shape[1]

    beside = swap(moments[:, 0], "clus", 1)
    *pieces, mine, mask, picks, coupling_near, evaluation_near = pick_slots(
        history,
        moments[:, 0],
        offsets,
        pair_sources,
        body_cluster[None],
        [coupling[0], evaluation],
        lag_count,
        lags_here,
    )
    pieces = [pieces[0]] + [turn(pieces[s], "lag", s) for s in range(1, lag_count)]
    pair = jnp.stack([mine, beside])
    gathered = [pair] + [swap(pair, "clus", t) for t in range(2, clus_count, 2)]
    near = bring_near(pair, kernel)
    far = far_rows(gathered, picks, coupling_near, evaluation_near)

    send = partial_sums(pieces, near, far, mask, 1)
    keep = partial_sums(pieces, near, far, mask, 0)
    middle = lag_count // 2
    sums, powers = {}, {}
    for h in (1, 0):
        total = keep[h] + swap(send[h], "clus", 1)
        kept = [total[i] for i in range(clus_count // 2)]
        bit = 2
        while bit < clus_count:
            came = [unpack(swap(pack(v, exponents(v)), "clus", bit)) for v in kept[1::2]]
            kept = [a + b for a, b in zip(kept[0::2], came)]
            bit *= 2
        sums[h] = kept[0]
        powers[h] = exponents(kept[0])
    owned = None
    for s in range(lag_count - 1, -1, -1):
        h, at = s // middle, (s % middle) * here
        part = sums[h][at : at + here]
        if s > 0:
            part = unpack(turn(pack(part, powers[h]), "lag", -s))
        owned = part if owned is None else owned + part
    return owned.astype(jnp.bfloat16)


def solution(mesh):
    in_specs = (
        P(None, ("farm", "lag"), "clus"),
        P("lag", "clus", None),
        P(None, ("farm", "clus"), None),
        P("clus", None, "lag", None, None),
        P(),
        P(),
        P(),
        P(),
    )
    out_specs = P(("farm", "lag"), "clus")
    return jax.shard_map(shards, mesh=mesh, in_specs=in_specs, out_specs=out_specs, check_vma=False)
```
